32 devices in a mesh: cam: 4 (over x, core), pt: 8 (over z, y).
Axes of the slice: x: 2, y: 2, z: 4, core: 2. Of those that a mesh axis runs over, the one named last changes fastest.
Arguments:
- right_side: float32 [9, 65536], P(None, ('cam', 'pt')), may hold values from -6 to 6
- cam_damping: float32 [9, 65536], P(None, ('cam', 'pt')), may hold values from 0.5 to 4
- point_damping: float32 [524288], P('pt'), may hold values from 0.1 to 1
- block_ids: int32 [4, 8, 64], P('cam', 'pt'), may hold values from 0 to 255, as said below
- slab_ids: int32 [4, 8, 64], P('cam', 'pt'), may hold values from 0 to 15
- cam_index: int32 [4, 8, 64, 4096], P('cam', 'pt'), may hold values from 0 to 63
- cam_jacobian: bfloat16 [4, 8, 64, 18, 4096], P('cam', 'pt'), may hold values from -0.59765625 to 0.59765625
- point_jacobian: bfloat16 [4, 8, 64, 6, 4096], P('cam', 'pt'), may hold values from -1.796875 to 1.796875
- pair_count: int32 [4, 8], P('cam', 'pt'), may hold values from 16 to 64, as said below
Outputs:
- solution: float32 [9, 65536], P(None, ('cam', 'pt'))
- residual: float32 [9, 65536], P(None, ('cam', 'pt'))
The draws below stay inside these ranges and needn't reach their ends.
Inputs may be any that keep to these rules, and one draw needn't show every extreme that they name: pair_count is 64 divided by a whole number from 1 to 4, rounded down; at least one device has all 64 slots used in every draw. The owner of a block is block_ids // 32; in every device's list at most 16 slots name blocks of one owner, and in every list some owner is named by exactly 16 slots.
All inputs are finite; a program needn't handle non-finite values.
Results may differ from the reference program's by a relative error of at most 0.0003.
Values sent between devices are 32-bit elements; how exact they have to be, the bound alone decides.
A program may use at most 128 MiB of HBM per device.

```python
import math
import jax
import jax.numpy as jnp
from jax import lax

BLOCK = 64
SLAB = 4096
ITERS = 2
BLK_DEV = 32
SLABS_PT = 16
PAIRS_DEV = 64
BLK_GRP = 256
CAP = 16
CAMERAS = 65536
POINTS = 524288
N_CAM = 4
N_PT = 8


def draw_pair_count(key, part):
    first_key, second_key = jax.random.split(key)
    divisor = jax.random.randint(first_key, (N_CAM * N_PT,), 1, 5)
    counts = PAIRS_DEV // divisor
    chosen = jax.random.randint(second_key, (), 0, N_CAM * N_PT)
    filled = jnp.where(jnp.arange(N_CAM * N_PT) == chosen, PAIRS_DEV, counts)
    return filled.reshape(N_CAM, N_PT).astype(jnp.int32)


def one_list(list_key):
    key_full, key_pick, key_order, key_local = jax.random.split(list_key, 4)
    busiest = jax.random.randint(key_full, (), 0, N_PT)
    others = (jnp.arange(N_PT - 1, dtype=jnp.int32) + busiest + 1) % N_PT
    pool = jax.random.permutation(key_pick, jnp.repeat(others, CAP))
    owners = jnp.concatenate([jnp.full((CAP,), busiest, jnp.int32), pool[:PAIRS_DEV - CAP]])
    owners = jax.random.permutation(key_order, owners)
    local = jax.random.randint(key_local, (PAIRS_DEV,), 0, BLK_DEV)
    return (owners * BLK_DEV + local).astype(jnp.int32)


def draw_block_ids(key, part):
    list_keys = jax.random.split(jax.random.fold_in(key, 17), N_CAM * N_PT)
    lists = jax.vmap(one_list)(list_keys)
    return lists.reshape(N_CAM, N_PT, PAIRS_DEV).astype(jnp.int32)


def plant(drawn, own_key, smallest, high):
    dims = drawn.shape
    index_at = [jax.random.randint(jax.random.fold_in(own_key, axis), (), 0, dims[axis]) for axis in range(len(dims))]
    drawn = drawn.at[tuple(index_at)].set(smallest)
    longest = dims.index(max(dims))
    index_at[longest] = (index_at[longest] + 1) % dims[longest]
    return drawn.at[tuple(index_at)].set(high)


def block_scale(rng, extent, cuts, smallest, largest):
    def one(position, shards_of):
        draws = jax.random.uniform(jax.random.fold_in(jax.random.fold_in(rng, 6), position), (shards_of,), jnp.float32, smallest / len(cuts), largest / len(cuts))
        return jnp.repeat(jnp.exp(draws), extent[position] // shards_of).reshape((-1,) + (1,) * (len(extent) - position - 1))

    loudness = one(*cuts[0])
    for cut in cuts[1:]:
        loudness = loudness * one(*cut)
    return loudness


def scatter_about(own_key, shape, spread, limit, cuts=(), held_as=jnp.bfloat16):
    result = spread * jax.random.normal(own_key, shape, jnp.float32)
    if cuts:
        result = result * block_scale(own_key, shape, cuts, -0.22, 0.18)
    return jnp.clip(result, -limit, limit).astype(held_as)


def setup_inputs(seed: int = 0) -> dict:
    streams_of = jax.random.split(jax.random.key(seed), 10)
    right_side = scatter_about(streams_of[0], (9, CAMERAS), 1.0, 6.0, ((1, 32),), jnp.float32)
    cam_damping = jnp.clip(jnp.exp(math.log(4.0) - 2.0794415 * jax.random.uniform(streams_of[1], (9, CAMERAS), jnp.float32) ** block_scale(streams_of[1], (9, CAMERAS), ((1, 32),), -0.2, 0.2)), 0.5, 4.0)
    point_damping = jnp.clip(jnp.exp(math.log(1.0) - 2.3025851 * jax.random.uniform(streams_of[2], (POINTS,), jnp.float32) ** block_scale(streams_of[2], (POINTS,), ((0, 8),), -0.2, 0.2)), 0.1, 1.0)
    block_ids = draw_block_ids(jax.random.fold_in(streams_of[9], 71), 0)
    slab_ids = plant(jax.random.randint(streams_of[4], (N_CAM, N_PT, PAIRS_DEV), 0, SLABS_PT), jax.random.fold_in(streams_of[4], 1), 0, SLABS_PT - 1).astype(jnp.int32)
    cam_index = plant(jax.random.randint(streams_of[5], (N_CAM, N_PT, PAIRS_DEV, SLAB), 0, BLOCK), jax.random.fold_in(streams_of[5], 1), 0, BLOCK - 1).astype(jnp.int32)
    cam_jacobian = scatter_about(streams_of[6], (N_CAM, N_PT, PAIRS_DEV, 18, SLAB), 0.1, 0.59765625, ((0, 4), (1, 8)))
    point_jacobian = scatter_about(streams_of[7], (N_CAM, N_PT, PAIRS_DEV, 6, SLAB), 0.3, 1.796875, ((0, 4), (1, 8)))
    pair_count = draw_pair_count(jax.random.fold_in(streams_of[9], 71), 0)
    return {"right_side": right_side, "cam_damping": cam_damping, "point_damping": point_damping, "block_ids": block_ids, "slab_ids": slab_ids, "cam_index": cam_index, "cam_jacobian": cam_jacobian, "point_jacobian": point_jacobian, "pair_count": pair_count}


HIGH = lax.Precision.HIGHEST


def hessian_terms(pt_jac):
    combos = [(0, 0), (0, 1), (0, 2), (1, 1), (1, 2), (2, 2)]
    return jnp.stack([jnp.sum(pt_jac[:, :, first].astype(jnp.float32) * pt_jac[:, :, second], axis=1) for first, second in combos], axis=1)


def collect(selector, terms):
    summed = jnp.einsum('ps,pkn->ksn', selector, terms, precision=HIGH)
    return summed.reshape(terms.shape[1], -1)


def invert_points(hess, damping):
    entry_xx = hess[0] + damping
    entry_xy = hess[1]
    entry_xz = hess[2]
    entry_yy = hess[3] + damping
    entry_yz = hess[4]
    entry_zz = hess[5] + damping
    cof_xx = entry_yy * entry_zz - entry_yz * entry_yz
    cof_xy = entry_xz * entry_yz - entry_xy * entry_zz
    cof_xz = entry_xy * entry_yz - entry_xz * entry_yy
    cof_yy = entry_xx * entry_zz - entry_xz * entry_xz
    cof_yz = entry_xy * entry_xz - entry_xx * entry_yz
    cof_zz = entry_xx * entry_yy - entry_xy * entry_xy
    determinant = entry_xx * cof_xx + entry_xy * cof_xy + entry_xz * cof_xz
    return jnp.stack([cof_xx, cof_xy, cof_xz, cof_yy, cof_yz, cof_zz]) / determinant


def apply_inverse(inverse, vector):
    out_x = inverse[0] * vector[0] + inverse[1] * vector[1] + inverse[2] * vector[2]
    out_y = inverse[1] * vector[0] + inverse[3] * vector[1] + inverse[4] * vector[2]
    out_z = inverse[2] * vector[0] + inverse[4] * vector[1] + inverse[5] * vector[2]
    return jnp.stack([out_x, out_y, out_z])


def project(cam_panel, blocks_here, index_here, cam_jac):
    grouped = cam_panel.reshape(9, -1, BLOCK).transpose(1, 0, 2)
    picked = grouped[blocks_here]
    at_camera = jnp.take_along_axis(picked, index_here[:, None, :], axis=2)
    return jnp.sum(cam_jac * at_camera[:, None], axis=2)


def reference(right_side, cam_damping, point_damping, block_ids, slab_ids, cam_index, cam_jacobian, point_jacobian, pair_count):
    devices_all = N_CAM * N_PT
    cam_grp = BLK_GRP * BLOCK
    npt = SLABS_PT * SLAB
    blocks_all = block_ids.reshape(devices_all, PAIRS_DEV)
    slabs_all = slab_ids.reshape(devices_all, PAIRS_DEV)
    index_all = cam_index.reshape(devices_all, PAIRS_DEV, SLAB)
    camjac_all = cam_jacobian.reshape(devices_all, PAIRS_DEV, 2, 9, SLAB)
    ptjac_all = point_jacobian.reshape(devices_all, PAIRS_DEV, 2, 3, SLAB)
    live_all = (jnp.arange(PAIRS_DEV, dtype=jnp.int32)[None, :] < pair_count.reshape(devices_all, 1)).astype(jnp.float32)
    slab_range = jnp.arange(SLABS_PT, dtype=jnp.int32)

    def selector_of(device):
        return (slabs_all[device][:, None] == slab_range[None, :]).astype(jnp.float32) * live_all[device][:, None]

    def hess_one(device):
        return collect(selector_of(device), hessian_terms(ptjac_all[device]))

    hess = lax.map(hess_one, jnp.arange(devices_all, dtype=jnp.int32))
    hess = jnp.sum(hess.reshape(N_CAM, N_PT, 6, npt), axis=0)
    inverse = jax.vmap(invert_points)(hess, point_damping.reshape(N_PT, npt))

    def schur(vector):
        groups = vector.reshape(9, N_CAM, cam_grp)

        def panel_of(device):
            return jnp.take(groups, device // N_PT, axis=1)

        def forward(device):
            projected = project(panel_of(device), blocks_all[device], index_all[device], camjac_all[device])
            pulled = jnp.sum(ptjac_all[device] * projected[:, :, None], axis=1)
            return collect(selector_of(device), pulled)

        point_parts = lax.map(forward, jnp.arange(devices_all, dtype=jnp.int32))
        point_sum = jnp.sum(point_parts.reshape(N_CAM, N_PT, 3, npt), axis=0)
        eliminated = jax.vmap(apply_inverse)(inverse, point_sum)

        def backward(device):
            cam_jac = camjac_all[device]
            pt_jac = ptjac_all[device]
            projected = project(panel_of(device), blocks_all[device], index_all[device], cam_jac)
            zpoint = jnp.take(eliminated, device % N_PT, axis=0).reshape(3, SLABS_PT, SLAB)
            pulled_back = jnp.moveaxis(zpoint[:, slabs_all[device], :], 0, 1)
            miss = projected - jnp.sum(pt_jac * pulled_back[:, None], axis=2)
            pushed = jnp.sum(cam_jac * miss[:, :, None], axis=1)
            flat_index = (jnp.arange(PAIRS_DEV, dtype=jnp.int32)[:, None] * BLOCK + index_all[device]).reshape(-1)
            values = pushed.transpose(0, 2, 1).reshape(-1, 9)
            cam_parts = jnp.zeros((PAIRS_DEV * BLOCK, 9), jnp.float32).at[flat_index].add(values)
            cam_parts = cam_parts.reshape(PAIRS_DEV, BLOCK, 9).transpose(0, 2, 1) * live_all[device][:, None, None]
            group_sum = jnp.zeros((BLK_GRP, 9, BLOCK), jnp.float32).at[blocks_all[device]].add(cam_parts)
            return group_sum.transpose(1, 0, 2).reshape(9, cam_grp)

        cam_all = lax.map(backward, jnp.arange(devices_all, dtype=jnp.int32))
        cam_all = jnp.sum(cam_all.reshape(N_CAM, N_PT, 9, cam_grp), axis=1)
        return cam_damping * vector + cam_all.transpose(1, 0, 2).reshape(9, CAMERAS)

    solution = jnp.zeros_like(right_side)
    residual = right_side
    direction = right_side
    norm_now = jnp.sum(residual * residual)
    for iteration in range(ITERS):
        image = schur(direction)
        step_size = norm_now / jnp.sum(direction * image)
        solution = solution + step_size * direction
        residual = residual - step_size * image
        norm_next = jnp.sum(residual * residual)
        direction = residual + (norm_next / norm_now) * direction
        norm_now = norm_next
    return solution, residual
```

```python
import functools

import jax
import jax.numpy as jnp
from jax import lax
from jax.experimental import pallas as pl
from jax.experimental.pallas import tpu as pltpu
from jax.sharding import PartitionSpec as P

BLOCK = 64
ITERS = 2
LANES = 128
STEP = 8
WIDTH = 512
F32 = jnp.float32
BF16 = jnp.bfloat16
VMEM_BYTES = 56 * 1024 * 1024


def pad_rows(value, rows):
    missing = rows - value.shape[0]
    return jnp.concatenate([value, jnp.zeros((missing, value.shape[1]), value.dtype)], axis=0)


def spread_rows(source, target):
    for j in range(STEP):
        target[pl.ds(j * 8, 8), :] = jnp.broadcast_to(source[j : j + 1, :], (8, source.shape[1]))


def row_ids(rows, cols):
    return lax.broadcasted_iota(jnp.int32, (rows, cols), 0)


def forward_kernel(
    first, blocks, slabs_of, count, cam_ref, idx_ref, jc_ref, jp_ref, y_ref, proj_ref, *rest
):
    if first:
        table, yacc, spread, hacc = rest
    else:
        table, yacc, spread = rest
    step = pl.program_id(0)
    owners, _, rows, _ = cam_ref.shape
    slab_len = jc_ref.shape[2]
    parts, _, slabs, part_len = y_ref.shape

    @pl.when(step == 0)
    def _():
        table[...] = jnp.zeros_like(table)
        yacc[...] = jnp.zeros_like(yacc)
        if first:
            hacc[...] = jnp.zeros_like(hacc)
        for owner in range(owners):
            for k in range(9):
                value = cam_ref[owner, k]
                table[pl.ds(owner * rows * 24 + k, rows, stride=24), :] = value
                table[pl.ds(owner * rows * 24 + 9 + k, rows, stride=24), :] = value

    spread_rows(idx_ref, spread)
    row24 = row_ids(24, LANES)
    row8 = row_ids(8, LANES)

    def slot(j, carry):
        place = step * STEP + j
        block = blocks[place]
        slab = slabs_of[place]
        offset = (block % 2) * BLOCK
        here = table[pl.ds(pl.multiple_of((block // 2) * 24, 8), 24), :]
        for start in range(0, slab_len, LANES):
            cols = pl.ds(start, LANES)
            spot = pl.ds(pl.multiple_of((start // LANES * slabs + slab) * 8, 8), 8)
            index = spread[pl.ds(pl.multiple_of(j * 8, 8), 8), cols] + offset
            index = jnp.concatenate([index] * 3, axis=0)
            at_camera = jnp.take_along_axis(here, index, axis=1, mode="promise_in_bounds")
            prod = pad_rows(jc_ref[j, :, cols].astype(F32), 24) * at_camera
            zero = jnp.zeros_like(prod[:8])
            mid = prod[8:16]
            first_row = row8 < 1
            part0 = prod[0:8] + jnp.where(first_row, mid, zero)
            part1 = jnp.where(first_row, zero, mid) + prod[16:24]
            proj0 = jnp.sum(part0, axis=0, keepdims=True)
            proj1 = jnp.sum(part1, axis=0, keepdims=True)
            proj_ref[j, 0:1, cols] = proj0
            proj_ref[j, 1:2, cols] = proj1
            jp = pad_rows(jp_ref[j, :, cols].astype(F32), 8)
            pulled = jp * jnp.where(row8 < 3, proj0, proj1)
            yacc[spot, :] += pulled + pltpu.roll(pulled, 5, 0)
            if first:
                same = jp * jp
                near = jp * pltpu.roll(jp, 7, 0)
                far = jp * pltpu.roll(jp, 6, 0)
                same = same + pltpu.roll(same, 5, 0)
                near = near + pltpu.roll(near, 5, 0)
                far = far + pltpu.roll(far, 5, 0)
                packed = jnp.where(
                    row8 < 3,
                    same,
                    jnp.where(row8 < 5, pltpu.roll(near, 3, 0), pltpu.roll(far, 5, 0)),
                )
                hacc[spot, :] += packed
        return carry

    lax.fori_loop(0, jnp.clip(count[0] - step * STEP, 0, STEP), slot, 0)

    @pl.when(step == pl.num_programs(0) - 1)
    def _():
        for chunk in range(slab_len // LANES):
            part, cols = chunk * LANES // part_len, pl.ds(chunk * LANES % part_len, LANES)
            for group in range(slabs // 8):
                top = (chunk * slabs + group * 8) * 8
                down = pl.ds(group * 8, 8)
                for k in range(3):
                    y_ref[part, k, down, cols] = yacc[pl.ds(top + k, 8, stride=8), :]
                if first:
                    for k in range(6):
                        y_ref[part, 3 + k, down, cols] = hacc[pl.ds(top + k, 8, stride=8), :]


def backward_kernel(
    blocks, slabs_of, count, z_ref, proj_ref, idx_ref, jc_ref, jp_ref, out_ref, zrows, acc, spread
):
    step = pl.program_id(0)
    owners, _, rows, _ = out_ref.shape
    slab_len = jc_ref.shape[2]
    parts, _, slabs, part_len = z_ref.shape

    @pl.when(step == 0)
    def _():
        zrows[...] = jnp.zeros_like(zrows)
        acc[...] = jnp.zeros_like(acc)
        for chunk in range(slab_len // LANES):
            part, cols = chunk * LANES // part_len, pl.ds(chunk * LANES % part_len, LANES)
            for group in range(slabs // 8):
                top = (chunk * slabs + group * 8) * 8
                for k in range(3):
                    value = z_ref[part, k, pl.ds(group * 8, 8), cols]
                    zrows[pl.ds(top + k, 8, stride=8), :] = value
                    zrows[pl.ds(top + 3 + k, 8, stride=8), :] = value

    spread_rows(idx_ref, spread)
    row24 = row_ids(24, LANES)
    row8 = row_ids(8, LANES)
    cams = row_ids(BLOCK, LANES)
    half = lax.broadcasted_iota(jnp.int32, (16, LANES), 1) // BLOCK

    def slot(j, carry):
        place = step * STEP + j
        block = blocks[place]
        slab = slabs_of[place]
        total = jnp.zeros((48, BLOCK), F32)
        for outer in range(0, slab_len, WIDTH):
            values = []
            hots = []
            for start in range(outer, outer + WIDTH, LANES):
                cols = pl.ds(start, LANES)
                jp = pad_rows(jp_ref[j, :, cols].astype(F32), 8)
                spot = pl.ds(pl.multiple_of((start // LANES * slabs + slab) * 8, 8), 8)
                q = jp * zrows[spot, :]
                low3 = jnp.where(row8 < 3, q, jnp.zeros_like(q))
                miss0 = proj_ref[j, 0:1, cols] - jnp.sum(low3, axis=0, keepdims=True)
                miss1 = proj_ref[j, 1:2, cols] - jnp.sum(q - low3, axis=0, keepdims=True)
                pushed = pad_rows(jc_ref[j, :, cols].astype(F32), 24) * jnp.where(
                    row24 < 9, miss0, miss1
                )
                rest = pushed - pushed.astype(BF16).astype(F32)
                values.append(jnp.concatenate([pushed, rest], axis=0).astype(BF16))
                index = spread[pl.ds(pl.multiple_of(j * 8, 8), 8), cols]
                index = jnp.concatenate([index] * (BLOCK // 8), axis=0)
                hots.append(jnp.where(cams == index, 1.0, 0.0).astype(BF16))
            total = total + lax.dot_general(
                jnp.concatenate(values, axis=1),
                jnp.concatenate(hots, axis=1),
                (((1,), (1,)), ((), ())),
                preferred_element_type=F32,
            )
        both = total[0:24] + total[24:48]
        sums = both + pltpu.roll(both, 15, 0)
        wide = jnp.concatenate([sums[0:16], sums[0:16]], axis=1)
        where = pl.ds(pl.multiple_of((block // 2) * 16, 16), 16)
        acc[where, :] += jnp.where(half == block % 2, wide, jnp.zeros_like(wide))
        return carry

    lax.fori_loop(0, jnp.clip(count[0] - step * STEP, 0, STEP), slot, 0)

    @pl.when(step == pl.num_programs(0) - 1)
    def _():
        for owner in range(owners):
            for k in range(9):
                out_ref[owner, k] = acc[pl.ds(owner * rows * 16 + k, rows, stride=16), :]


def whole(shape):
    return pl.BlockSpec(shape, lambda i, *_: (0,) * len(shape))


def data_specs(pairs, slab_len):
    return [
        pl.BlockSpec((STEP, slab_len), lambda i, *_: (i, 0)),
        pl.BlockSpec((STEP, 18, slab_len), lambda i, *_: (i, 0, 0)),
        pl.BlockSpec((STEP, 6, slab_len), lambda i, *_: (i, 0, 0)),
    ]


def forward(first, lists, cams, idx, jc, jp, parts, slabs):
    pairs, slab_len = idx.shape
    owners, _, rows, _ = cams.shape
    part_len = slab_len // parts
    y_shape = (parts, 9 if first else 3, slabs, part_len)
    proj_spec = pl.BlockSpec((STEP, 2, slab_len), lambda i, *_: (i, 0, 0))
    out_shape = [
        jax.ShapeDtypeStruct(y_shape, F32),
        jax.ShapeDtypeStruct((pairs, 2, slab_len), F32),
    ]
    out_specs = [whole(y_shape), proj_spec]
    scratch = [
        pltpu.VMEM((owners * rows * 24, LANES), F32),
        pltpu.VMEM((slabs * 8 * (slab_len // LANES), LANES), F32),
        pltpu.VMEM((STEP * 8, slab_len), jnp.int32),
    ]
    if first:
        scratch.append(pltpu.VMEM((slabs * 8 * (slab_len // LANES), LANES), F32))
    return pl.pallas_call(
        functools.partial(forward_kernel, first),
        name="forward_first" if first else "forward_next",
        out_shape=out_shape,
        grid_spec=pltpu.PrefetchScalarGridSpec(
            num_scalar_prefetch=3,
            grid=(pairs // STEP,),
            in_specs=[whole(cams.shape)] + data_specs(pairs, slab_len),
            out_specs=out_specs,
            scratch_shapes=scratch,
        ),
        compiler_params=pltpu.CompilerParams(
            dimension_semantics=("arbitrary",), vmem_limit_bytes=VMEM_BYTES
        ),
    )(*lists, cams, idx, jc, jp)


def backward(lists, z, proj, idx, jc, jp, owners, rows):
    pairs, slab_len = idx.shape
    slabs = z.shape[2]
    out_shape = (owners, 9, rows, LANES)
    proj_spec = pl.BlockSpec((STEP, 2, slab_len), lambda i, *_: (i, 0, 0))
    return pl.pallas_call(
        backward_kernel,
        name="backward",
        out_shape=jax.ShapeDtypeStruct(out_shape, F32),
        grid_spec=pltpu.PrefetchScalarGridSpec(
            num_scalar_prefetch=3,
            grid=(pairs // STEP,),
            in_specs=[whole(z.shape), proj_spec] + data_specs(pairs, slab_len),
            out_specs=whole(out_shape),
            scratch_shapes=[
                pltpu.VMEM((slabs * 8 * (slab_len // LANES), LANES), F32),
                pltpu.VMEM((owners * rows * 16, LANES), F32),
                pltpu.VMEM((STEP * 8, slab_len), jnp.int32),
            ],
        ),
        compiler_params=pltpu.CompilerParams(
            dimension_semantics=("arbitrary",), vmem_limit_bytes=VMEM_BYTES
        ),
    )(*lists, z, proj, idx, jc, jp)


def swap_kernel(axis, gather, x_ref, out_ref, slots, send_sem, recv_sem):
    peers = lax.axis_size(axis)
    me = lax.axis_index(axis)
    barrier = pltpu.get_barrier_semaphore()
    for hop in range(1, peers):
        pl.semaphore_signal(
            barrier,
            inc=1,
            device_id={axis: lax.rem(me + hop, peers)},
            device_id_type=pl.DeviceIdType.MESH,
        )
    pl.semaphore_wait(barrier, peers - 1)
    copies = []
    for hop in range(1, peers):
        peer = lax.rem(me + hop, peers)
        copy = pltpu.make_async_remote_copy(
            src_ref=x_ref if gather else x_ref.at[peer],
            dst_ref=slots.at[hop - 1],
            send_sem=send_sem.at[hop - 1],
            recv_sem=recv_sem.at[hop - 1],
            device_id={axis: peer},
            device_id_type=pl.DeviceIdType.MESH,
        )
        copy.start()
        copies.append(copy)
    if gather:
        out_ref[me] = x_ref[...]
        for hop in range(1, peers):
            copies[hop - 1].wait()
            out_ref[lax.rem(me + peers - hop, peers)] = slots[hop - 1]
    else:
        for copy in copies:
            copy.wait()
        for k in range(out_ref.shape[0]):
            total = x_ref[me, k]
            for hop in range(1, peers):
                total = total + slots[hop - 1, k]
            out_ref[k] = total


def swap(value, axis, gather, ident):
    peers = lax.axis_size(axis)
    piece = value.shape if gather else value.shape[1:]
    out = (peers,) + piece if gather else piece
    return pl.pallas_call(
        functools.partial(swap_kernel, axis, gather),
        name=("gather_" if gather else "scatter_") + axis,
        out_shape=jax.ShapeDtypeStruct(out, F32),
        in_specs=[pl.BlockSpec(memory_space=pltpu.VMEM)],
        out_specs=pl.BlockSpec(memory_space=pltpu.VMEM),
        scratch_shapes=[
            pltpu.VMEM((peers - 1,) + piece, F32),
            pltpu.SemaphoreType.DMA((peers - 1,)),
            pltpu.SemaphoreType.DMA((peers - 1,)),
        ],
        compiler_params=pltpu.CompilerParams(
            collective_id=ident, has_side_effects=True, vmem_limit_bytes=24 * 1024 * 1024
        ),
    )(value)


def tile_of(values):
    return jnp.broadcast_to(jnp.stack(values)[:, None, None], (len(values), 8, LANES))


def over_cam(values):
    padded = values + [jnp.zeros((), F32)] * (2 - len(values))
    return jnp.sum(swap(tile_of(padded), "cam", True, 6)[:, :, 0, 0], axis=0)


def over_pt(value):
    return jnp.sum(swap(tile_of([value]), "pt", True, 5)[:, 0, 0, 0])


def invert_points(hess, damping):
    entry_xx = hess[0] + damping
    entry_yy = hess[1] + damping
    entry_zz = hess[2] + damping
    entry_xy = hess[3]
    entry_yz = hess[4]
    entry_xz = hess[5]
    cof_xx = entry_yy * entry_zz - entry_yz * entry_yz
    cof_xy = entry_xz * entry_yz - entry_xy * entry_zz
    cof_xz = entry_xy * entry_yz - entry_xz * entry_yy
    cof_yy = entry_xx * entry_zz - entry_xz * entry_xz
    cof_yz = entry_xy * entry_xz - entry_xx * entry_yz
    cof_zz = entry_xx * entry_yy - entry_xy * entry_xy
    determinant = entry_xx * cof_xx + entry_xy * cof_xy + entry_xz * cof_xz
    return [
        cof / determinant for cof in (cof_xx, cof_xy, cof_xz, cof_yy, cof_yz, cof_zz)
    ]


def apply_inverse(inverse, vector):
    out_x = inverse[0] * vector[0] + inverse[1] * vector[1] + inverse[2] * vector[2]
    out_y = inverse[1] * vector[0] + inverse[3] * vector[1] + inverse[4] * vector[2]
    out_z = inverse[2] * vector[0] + inverse[4] * vector[1] + inverse[5] * vector[2]
    return jnp.stack([out_x, out_y, out_z])


def per_device(
    right_side,
    cam_damping,
    point_damping,
    block_ids,
    slab_ids,
    cam_index,
    cam_jacobian,
    point_jacobian,
    pair_count,
):
    pairs = block_ids.shape[2]
    slab_len = cam_index.shape[3]
    slabs = point_damping.shape[0] // slab_len
    cam_dev = right_side.shape[1]
    rows = cam_dev // LANES
    owners = lax.axis_size("pt")
    parts = lax.axis_size("cam")
    part_len = slab_len // parts
    lists = (block_ids.reshape(pairs), slab_ids.reshape(pairs), pair_count.reshape(1))
    idx = cam_index.reshape(pairs, slab_len)
    jc = cam_jacobian.reshape(pairs, 18, slab_len)
    jp = point_jacobian.reshape(pairs, 6, slab_len)
    residual = right_side.reshape(9, rows, LANES)
    damping = cam_damping.reshape(9, rows, LANES)
    part = lax.axis_index("cam")
    point_damp = lax.dynamic_slice_in_dim(
        point_damping.reshape(slabs, slab_len), part * part_len, part_len, 1
    )
    direction = residual
    answer = jnp.zeros_like(residual)
    cams = swap(direction, "pt", True, 0)
    norm_group = jnp.sum(cams * cams)
    norm_now = None
    inverse = None
    for iteration in range(ITERS):
        if iteration == 0:
            y, proj = forward(True, lists, cams, idx, jc, jp, parts, slabs)
            merged = swap(y, "cam", False, 1)
            pulled = merged[:3]
            inverse = invert_points(merged[3:], point_damp)
        else:
            y, proj = forward(False, lists, cams, idx, jc, jp, parts, slabs)
            pulled = swap(y, "cam", False, 2)
        z = swap(apply_inverse(inverse, pulled), "cam", True, 3)
        sums = backward(lists, z, proj, idx, jc, jp, owners, rows)
        image = damping * direction + swap(sums, "pt", False, 4)
        curve = over_pt(jnp.sum(direction * image))
        if iteration == 0:
            both = over_cam([curve, norm_group])
            curve, norm_now = both[0], both[1]
        else:
            curve = over_cam([curve])[0]
        step_size = norm_now / curve
        answer = answer + step_size * direction
        residual = residual - step_size * image
        if iteration + 1 < ITERS:
            group = swap(residual, "pt", True, 0)
            norm_next = over_cam([jnp.sum(group * group)])[0]
            ratio = norm_next / norm_now
            cams = group + ratio * cams
            direction = residual + ratio * direction
            norm_now = norm_next
    return answer.reshape(9, cam_dev), residual.reshape(9, cam_dev)


def solution(mesh):
    in_specs = (
        P(None, ("cam", "pt")),
        P(None, ("cam", "pt")),
        P("pt"),
        P("cam", "pt", None),
        P("cam", "pt", None),
        P("cam", "pt", None, None),
        P("cam", "pt", None, None, None),
        P("cam", "pt", None, None, None),
        P("cam", "pt"),
    )
    out_specs = (P(None, ("cam", "pt")), P(None, ("cam", "pt")))
    return jax.shard_map(
        per_device, mesh=mesh, in_specs=in_specs, out_specs=out_specs, check_vma=False
    )
```

```python
import functools

import jax
import jax.numpy as jnp
from jax import lax
from jax.experimental import pallas as pl
from jax.experimental.pallas import tpu as pltpu
from jax.sharding import PartitionSpec as P

BLOCK = 64
ITERS = 2
LANES = 128
STEP = 8
WIDTH = 512
F32 = jnp.float32
BF16 = jnp.bfloat16
VMEM_BYTES = 56 * 1024 * 1024


def pad_rows(value, rows):
    missing = rows - value.shape[0]
    return jnp.concatenate([value, jnp.zeros((missing, value.shape[1]), value.dtype)], axis=0)


def spread_rows(source, target):
    for j in range(STEP):
        target[pl.ds(j * 8, 8), :] = jnp.broadcast_to(source[j : j + 1, :], (8, source.shape[1]))


def row_ids(rows, cols):
    return lax.broadcasted_iota(jnp.int32, (rows, cols), 0)


def forward_kernel(
    first, blocks, slabs_of, count, cam_ref, idx_ref, jc_ref, jp_ref, y_ref, proj_ref, *rest
):
    table, yacc, stage, tables, shift = rest
    step = pl.program_id(0)
    owners, _, rows, _ = cam_ref.shape
    slab_len = jc_ref.shape[2]
    parts, fields, slabs, part_len = y_ref.shape
    tall = 16 if first else 8

    @pl.when(step == 0)
    def _():
        table[...] = jnp.zeros_like(table)
        yacc[...] = jnp.zeros_like(yacc)
        stage[...] = jnp.zeros_like(stage)
        for owner in range(owners):
            for k in range(9):
                table[pl.ds(owner * rows * 16 + k, rows, stride=16), :] = cam_ref[owner, k]

    @pl.when(step * STEP < count[0])
    def _():
        for j in range(STEP):
            block = blocks[step * STEP + j]
            here = table[pl.ds(pl.multiple_of((block // 2) * 16, 16), 16), :]
            tables[pl.ds(j, 16, stride=8), :] = here
            shift[j : j + 1, :] = jnp.full((1, LANES), (block % 2) * BLOCK, jnp.int32)
        for chunk in range(slab_len // LANES):
            cols = pl.ds(chunk * LANES, LANES)
            index = idx_ref[:, cols] + shift[...]
            proj = [None, None]
            for k in range(9):
                at_camera = jnp.take_along_axis(
                    tables[pl.ds(k * 8, 8), :], index, axis=1, mode="promise_in_bounds"
                )
                for i in range(2):
                    term = jc_ref[9 * i + k, :, cols].astype(F32) * at_camera
                    proj[i] = term if k == 0 else proj[i] + term
            jp = [jp_ref[k, :, cols].astype(F32) for k in range(6)]
            made = [jp[k] * proj[0] + jp[3 + k] * proj[1] for k in range(3)]
            if first:
                pairs = [(0, 0), (1, 1), (2, 2), (0, 1), (1, 2), (0, 2)]
                made += [jp[a] * jp[b] + jp[3 + a] * jp[3 + b] for a, b in pairs]
            for i in range(2):
                proj_ref[i, :, cols] = proj[i]
            for k, value in enumerate(made):
                stage[pl.ds(chunk * 128 + k, 8, stride=16), :] = value

    def slot(j, carry):
        slab = slabs_of[step * STEP + j]
        for chunk in range(slab_len // LANES):
            spot = pl.ds(pl.multiple_of((chunk * slabs + slab) * tall, 8), tall)
            yacc[spot, :] += stage[pl.ds(pl.multiple_of(chunk * 128 + j * 16, 16), tall), :]
        return carry

    lax.fori_loop(0, jnp.clip(count[0] - step * STEP, 0, STEP), slot, 0)

    @pl.when(step == pl.num_programs(0) - 1)
    def _():
        for chunk in range(slab_len // LANES):
            part, cols = chunk * LANES // part_len, pl.ds(chunk * LANES % part_len, LANES)
            for group in range(slabs // 8):
                top = (chunk * slabs + group * 8) * tall
                for k in range(fields):
                    y_ref[part, k, pl.ds(group * 8, 8), cols] = yacc[
                        pl.ds(top + k, 8, stride=tall), :
                    ]


def backward_kernel(
    blocks, slabs_of, count, z_ref, proj_ref, idx_ref, jc_ref, jp_ref, out_ref,
    zrows, acc, spread, stage, zslot,
):
    step = pl.program_id(0)
    owners, _, rows, _ = out_ref.shape
    slab_len = jc_ref.shape[2]
    parts, _, slabs, part_len = z_ref.shape

    @pl.when(step == 0)
    def _():
        zrows[...] = jnp.zeros_like(zrows)
        acc[...] = jnp.zeros_like(acc)
        stage[...] = jnp.zeros_like(stage)
        for chunk in range(slab_len // LANES):
            part, cols = chunk * LANES // part_len, pl.ds(chunk * LANES % part_len, LANES)
            for group in range(slabs // 8):
                top = (chunk * slabs + group * 8) * 8
                for k in range(3):
                    zrows[pl.ds(top + k, 8, stride=8), :] = z_ref[
                        part, k, pl.ds(group * 8, 8), cols
                    ]

    @pl.when(step * STEP < count[0])
    def _():
        spread_rows(idx_ref, spread)
        for j in range(STEP):
            slab = slabs_of[step * STEP + j]
            for chunk in range(slab_len // LANES):
                spot = pl.ds(pl.multiple_of((chunk * slabs + slab) * 8, 8), 8)
                zslot[pl.ds(chunk * 64 + j, 8, stride=8), :] = zrows[spot, :]
        for chunk in range(slab_len // LANES):
            cols = pl.ds(chunk * LANES, LANES)
            miss = [proj_ref[i, :, cols] for i in range(2)]
            for k in range(3):
                z = zslot[pl.ds(chunk * 64 + k * 8, 8), :]
                for i in range(2):
                    miss[i] = miss[i] - jp_ref[3 * i + k, :, cols].astype(F32) * z
            for k in range(9):
                stage[pl.ds(chunk * 128 + k, 8, stride=16), :] = (
                    jc_ref[k, :, cols].astype(F32) * miss[0]
                    + jc_ref[9 + k, :, cols].astype(F32) * miss[1]
                )

    cams = row_ids(BLOCK, LANES)
    half = lax.broadcasted_iota(jnp.int32, (16, LANES), 1) // BLOCK

    def slot(j, carry):
        block = blocks[step * STEP + j]
        total = jnp.zeros((32, BLOCK), F32)
        for outer in range(0, slab_len, WIDTH):
            values = []
            hots = []
            for start in range(outer, outer + WIDTH, LANES):
                cols = pl.ds(start, LANES)
                pushed = stage[pl.ds(pl.multiple_of(start + j * 16, 16), 16), :]
                rest = pushed - pushed.astype(BF16).astype(F32)
                values.append(jnp.concatenate([pushed, rest], axis=0).astype(BF16))
                index = spread[pl.ds(pl.multiple_of(j * 8, 8), 8), cols]
                index = jnp.concatenate([index] * (BLOCK // 8), axis=0)
                hots.append(jnp.where(cams == index, 1.0, 0.0).astype(BF16))
            total = total + lax.dot_general(
                jnp.concatenate(values, axis=1),
                jnp.concatenate(hots, axis=1),
                (((1,), (1,)), ((), ())),
                preferred_element_type=F32,
            )
        sums = total[0:16] + total[16:32]
        wide = jnp.concatenate([sums, sums], axis=1)
        where = pl.ds(pl.multiple_of((block // 2) * 16, 16), 16)
        acc[where, :] += jnp.where(half == block % 2, wide, jnp.zeros_like(wide))
        return carry

    lax.fori_loop(0, jnp.clip(count[0] - step * STEP, 0, STEP), slot, 0)

    @pl.when(step == pl.num_programs(0) - 1)
    def _():
        for owner in range(owners):
            for k in range(9):
                out_ref[owner, k] = acc[pl.ds(owner * rows * 16 + k, rows, stride=16), :]


def whole(shape):
    return pl.BlockSpec(shape, lambda i, *_: (0,) * len(shape))


def data_specs(pairs, slab_len):
    return [
        pl.BlockSpec((STEP, slab_len), lambda i, *_: (i, 0)),
        pl.BlockSpec((18, STEP, slab_len), lambda i, *_: (0, i, 0)),
        pl.BlockSpec((6, STEP, slab_len), lambda i, *_: (0, i, 0)),
    ]


def forward(first, lists, cams, idx, jc, jp, parts, slabs):
    pairs, slab_len = idx.shape
    owners, _, rows, _ = cams.shape
    part_len = slab_len // parts
    y_shape = (parts, 9 if first else 3, slabs, part_len)
    proj_spec = pl.BlockSpec((2, STEP, slab_len), lambda i, *_: (0, i, 0))
    out_shape = [
        jax.ShapeDtypeStruct(y_shape, F32),
        jax.ShapeDtypeStruct((2, pairs, slab_len), F32),
    ]
    out_specs = [whole(y_shape), proj_spec]
    scratch = [
        pltpu.VMEM((owners * rows * 16, LANES), F32),
        pltpu.VMEM((slabs * (16 if first else 8) * (slab_len // LANES), LANES), F32),
        pltpu.VMEM((slab_len, LANES), F32),
        pltpu.VMEM((16 * STEP, LANES), F32),
        pltpu.VMEM((STEP, LANES), jnp.int32),
    ]
    return pl.pallas_call(
        functools.partial(forward_kernel, first),
        name="forward_first" if first else "forward_next",
        out_shape=out_shape,
        grid_spec=pltpu.PrefetchScalarGridSpec(
            num_scalar_prefetch=3,
            grid=(pairs // STEP,),
            in_specs=[whole(cams.shape)] + data_specs(pairs, slab_len),
            out_specs=out_specs,
            scratch_shapes=scratch,
        ),
        compiler_params=pltpu.CompilerParams(
            dimension_semantics=("arbitrary",), vmem_limit_bytes=VMEM_BYTES
        ),
    )(*lists, cams, idx, jc, jp)


def backward(lists, z, proj, idx, jc, jp, owners, rows):
    pairs, slab_len = idx.shape
    slabs = z.shape[2]
    out_shape = (owners, 9, rows, LANES)
    proj_spec = pl.BlockSpec((2, STEP, slab_len), lambda i, *_: (0, i, 0))
    return pl.pallas_call(
        backward_kernel,
        name="backward",
        out_shape=jax.ShapeDtypeStruct(out_shape, F32),
        grid_spec=pltpu.PrefetchScalarGridSpec(
            num_scalar_prefetch=3,
            grid=(pairs // STEP,),
            in_specs=[whole(z.shape), proj_spec] + data_specs(pairs, slab_len),
            out_specs=whole(out_shape),
            scratch_shapes=[
                pltpu.VMEM((slabs * 8 * (slab_len // LANES), LANES), F32),
                pltpu.VMEM((owners * rows * 16, LANES), F32),
                pltpu.VMEM((STEP * 8, slab_len), jnp.int32),
                pltpu.VMEM((slab_len, LANES), F32),
                pltpu.VMEM((slab_len // 2, LANES), F32),
            ],
        ),
        compiler_params=pltpu.CompilerParams(
            dimension_semantics=("arbitrary",), vmem_limit_bytes=VMEM_BYTES
        ),
    )(*lists, z, proj, idx, jc, jp)


def swap_kernel(axis, gather, x_ref, out_ref, slots, send_sem, recv_sem):
    peers = lax.axis_size(axis)
    me = lax.axis_index(axis)
    barrier = pltpu.get_barrier_semaphore()
    for hop in range(1, peers):
        pl.semaphore_signal(
            barrier,
            inc=1,
            device_id={axis: lax.rem(me + hop, peers)},
            device_id_type=pl.DeviceIdType.MESH,
        )
    pl.semaphore_wait(barrier, peers - 1)
    copies = []
    for hop in range(1, peers):
        peer = lax.rem(me + hop, peers)
        copy = pltpu.make_async_remote_copy(
            src_ref=x_ref if gather else x_ref.at[peer],
            dst_ref=slots.at[hop - 1],
            send_sem=send_sem.at[hop - 1],
            recv_sem=recv_sem.at[hop - 1],
            device_id={axis: peer},
            device_id_type=pl.DeviceIdType.MESH,
        )
        copy.start()
        copies.append(copy)
    if gather:
        out_ref[me] = x_ref[...]
        for hop in range(1, peers):
            copies[hop - 1].wait()
            out_ref[lax.rem(me + peers - hop, peers)] = slots[hop - 1]
    else:
        for copy in copies:
            copy.wait()
        for k in range(out_ref.shape[0]):
            total = x_ref[me, k]
            for hop in range(1, peers):
                total = total + slots[hop - 1, k]
            out_ref[k] = total


def swap(value, axis, gather, ident):
    peers = lax.axis_size(axis)
    piece = value.shape if gather else value.shape[1:]
    out = (peers,) + piece if gather else piece
    return pl.pallas_call(
        functools.partial(swap_kernel, axis, gather),
        name=("gather_" if gather else "scatter_") + axis,
        out_shape=jax.ShapeDtypeStruct(out, F32),
        in_specs=[pl.BlockSpec(memory_space=pltpu.VMEM)],
        out_specs=pl.BlockSpec(memory_space=pltpu.VMEM),
        scratch_shapes=[
            pltpu.VMEM((peers - 1,) + piece, F32),
            pltpu.SemaphoreType.DMA((peers - 1,)),
            pltpu.SemaphoreType.DMA((peers - 1,)),
        ],
        compiler_params=pltpu.CompilerParams(
            collective_id=ident, has_side_effects=True, vmem_limit_bytes=24 * 1024 * 1024
        ),
    )(value)


def tile_of(values):
    return jnp.broadcast_to(jnp.stack(values)[:, None, None], (len(values), 8, LANES))


def over_cam(values):
    padded = values + [jnp.zeros((), F32)] * (2 - len(values))
    return jnp.sum(swap(tile_of(padded), "cam", True, 6)[:, :, 0, 0], axis=0)


def over_pt(value):
    return jnp.sum(swap(tile_of([value]), "pt", True, 5)[:, 0, 0, 0])


def invert_points(hess, damping):
    entry_xx = hess[0] + damping
    entry_yy = hess[1] + damping
    entry_zz = hess[2] + damping
    entry_xy = hess[3]
    entry_yz = hess[4]
    entry_xz = hess[5]
    cof_xx = entry_yy * entry_zz - entry_yz * entry_yz
    cof_xy = entry_xz * entry_yz - entry_xy * entry_zz
    cof_xz = entry_xy * entry_yz - entry_xz * entry_yy
    cof_yy = entry_xx * entry_zz - entry_xz * entry_xz
    cof_yz = entry_xy * entry_xz - entry_xx * entry_yz
    cof_zz = entry_xx * entry_yy - entry_xy * entry_xy
    determinant = entry_xx * cof_xx + entry_xy * cof_xy + entry_xz * cof_xz
    return [
        cof / determinant for cof in (cof_xx, cof_xy, cof_xz, cof_yy, cof_yz, cof_zz)
    ]


def apply_inverse(inverse, vector):
    out_x = inverse[0] * vector[0] + inverse[1] * vector[1] + inverse[2] * vector[2]
    out_y = inverse[1] * vector[0] + inverse[3] * vector[1] + inverse[4] * vector[2]
    out_z = inverse[2] * vector[0] + inverse[4] * vector[1] + inverse[5] * vector[2]
    return jnp.stack([out_x, out_y, out_z])


def per_device(
    right_side,
    cam_damping,
    point_damping,
    block_ids,
    slab_ids,
    cam_index,
    cam_jacobian,
    point_jacobian,
    pair_count,
):
    pairs = block_ids.shape[2]
    slab_len = cam_index.shape[3]
    slabs = point_damping.shape[0] // slab_len
    cam_dev = right_side.shape[1]
    rows = cam_dev // LANES
    owners = lax.axis_size("pt")
    parts = lax.axis_size("cam")
    part_len = slab_len // parts
    lists = (block_ids.reshape(pairs), slab_ids.reshape(pairs), pair_count.reshape(1))
    idx = cam_index.reshape(pairs, slab_len)
    jc = cam_jacobian.reshape(pairs, 18, slab_len).transpose(1, 0, 2)
    jp = point_jacobian.reshape(pairs, 6, slab_len).transpose(1, 0, 2)
    residual = right_side.reshape(9, rows, LANES)
    damping = cam_damping.reshape(9, rows, LANES)
    part = lax.axis_index("cam")
    point_damp = lax.dynamic_slice_in_dim(
        point_damping.reshape(slabs, slab_len), part * part_len, part_len, 1
    )
    direction = residual
    answer = jnp.zeros_like(residual)
    cams = swap(direction, "pt", True, 0)
    norm_group = jnp.sum(cams * cams)
    norm_now = None
    inverse = None
    for iteration in range(ITERS):
        if iteration == 0:
            y, proj = forward(True, lists, cams, idx, jc, jp, parts, slabs)
            merged = swap(y, "cam", False, 1)
            pulled = merged[:3]
            inverse = invert_points(merged[3:], point_damp)
        else:
            y, proj = forward(False, lists, cams, idx, jc, jp, parts, slabs)
            pulled = swap(y, "cam", False, 2)
        z = swap(apply_inverse(inverse, pulled), "cam", True, 3)
        sums = backward(lists, z, proj, idx, jc, jp, owners, rows)
        image = damping * direction + swap(sums, "pt", False, 4)
        curve = over_pt(jnp.sum(direction * image))
        if iteration == 0:
            both = over_cam([curve, norm_group])
            curve, norm_now = both[0], both[1]
        else:
            curve = over_cam([curve])[0]
        step_size = norm_now / curve
        answer = answer + step_size * direction
        residual = residual - step_size * image
        if iteration + 1 < ITERS:
            group = swap(residual, "pt", True, 0)
            norm_next = over_cam([jnp.sum(group * group)])[0]
            ratio = norm_next / norm_now
            cams = group + ratio * cams
            direction = residual + ratio * direction
            norm_now = norm_next
    return answer.reshape(9, cam_dev), residual.reshape(9, cam_dev)


def solution(mesh):
    in_specs = (
        P(None, ("cam", "pt")),
        P(None, ("cam", "pt")),
        P("pt"),
        P("cam", "pt", None),
        P("cam", "pt", None),
        P("cam", "pt", None, None),
        P("cam", "pt", None, None, None),
        P("cam", "pt", None, None, None),
        P("cam", "pt"),
    )
    out_specs = (P(None, ("cam", "pt")), P(None, ("cam", "pt")))
    return jax.shard_map(
        per_device, mesh=mesh, in_specs=in_specs, out_specs=out_specs, check_vma=False
    )
```
